32 devices in a mesh: row: 8 (over z, x), col: 4 (over y, core).
Axes of the slice: x: 2, y: 2, z: 4, core: 2. Of those that a mesh axis runs over, the one named last changes fastest.
Arguments:
- events: bfloat16 [2048, 256], P(('row', 'col')), may hold values from -6 to 6
- timestamps: int32 [2048], replicated, may hold values from 0 to 8384512, as said below
- norm_gain: float32 [256], replicated, may hold values from 0.1 to 1.9
- w_in: bfloat16 [256, 1024], replicated, may hold values from -0.375 to 0.375
- rel_bias: float32 [2, 24], replicated, may hold values from -2 to 2
- out_gain: float32 [256], replicated, may hold values from 0.1 to 1.9
- w_out: bfloat16 [256, 256], replicated, may hold values from -0.75 to 0.75
Outputs:
- output: bfloat16 [2048, 256], P(('row', 'col'))
The draws below stay inside these ranges and needn't reach their ends.
Inputs may be any that keep to these rules, and one draw needn't show every extreme that they name: `timestamps`: nondecreasing along the events, the first one 0 and the last one 4096 * 2047.
All inputs are finite; a program needn't handle non-finite values.
Results may differ from the reference program's by a relative error of at most 0.006.
Values may be sent and summed in bfloat16 or wider, within the bound.
A program may use at most 64 MiB of HBM per device.

```python
import math
import jax
import jax.numpy as jnp
from jax import lax

D = 256
HEADS = 2
HEAD = 128
BUCKETS = 24
SEQ = 2048
QB = 256


def draw_timestamps(key, part):
    short_key, long_key, pick_key = jax.random.split(key, 3)
    short_gap = jax.random.randint(short_key, (SEQ,), 0, 8)
    long_gap = jax.random.randint(long_key, (SEQ,), 0, 4096)
    session = jax.random.randint(pick_key, (SEQ,), 0, 16) == 0
    time_gaps = jnp.where(session, long_gap, short_gap)
    time_gaps = jnp.where(jnp.arange(SEQ) == 0, 0, time_gaps)
    stamps = jnp.cumsum(time_gaps).astype(jnp.int32)
    last_time = jnp.int32(4096 * (SEQ - 1))
    return jnp.where(jnp.arange(SEQ) == SEQ - 1, last_time, stamps).astype(jnp.int32)


def block_scale(key, shape, shards, least, high):
    def one(dim, parts):
        heights = jax.random.uniform(jax.random.fold_in(jax.random.fold_in(key, 6), dim), (parts,), jnp.float32, least / len(shards), high / len(shards))
        return jnp.repeat(jnp.exp(heights), shape[dim] // parts).reshape((-1,) + (1,) * (len(shape) - dim - 1))

    factor_of = one(*shards[0])
    for cut in shards[1:]:
        factor_of = factor_of * one(*cut)
    return factor_of


def scatter_about(rng, shape, deviation, most, cuts=(), kind=jnp.bfloat16):
    array = deviation * jax.random.normal(rng, shape, jnp.float32)
    if cuts:
        array = array * block_scale(rng, shape, cuts, -0.22, 0.18)
    return jnp.clip(array, -most, most).astype(kind)


def setup_inputs(seed: int = 0) -> dict:
    streams_of = jax.random.split(jax.random.key(seed), 8)
    return {
        "events": scatter_about(streams_of[0], (SEQ, D), 1.0, 6.0, ((0, 32),)),
        "timestamps": draw_timestamps(jax.random.fold_in(streams_of[7], 71), 0),
        "norm_gain": jnp.clip(1.0 + 0.18 * jax.random.normal(streams_of[2], (D,), jnp.float32), 0.1, 1.9),
        "w_in": scatter_about(streams_of[3], (D, 4 * D), D ** -0.5, 0.375),
        "rel_bias": jnp.clip(jax.random.uniform(streams_of[4], (HEADS, BUCKETS), jnp.float32, -2.0, 2.0), -2.0, 2.0),
        "out_gain": jnp.clip(1.0 + 0.18 * jax.random.normal(streams_of[5], (D,), jnp.float32), 0.1, 1.9),
        "w_out": scatter_about(streams_of[6], (D, D), (D // 4) ** -0.5, 0.75),
    }


def layer_norm(row_values, gain_vec):
    center = row_values - lax.optimization_barrier(jnp.mean(row_values, axis=-1, keepdims=True))
    variance = lax.optimization_barrier(jnp.mean(center * center, axis=-1, keepdims=True))
    return center * lax.rsqrt(variance + 1e-05) * gain_vec

def bucket_of(time_delta):
    bucket = jnp.zeros(time_delta.shape, jnp.int32)
    for level_idx in range(BUCKETS - 1):
        bucket = bucket + (time_delta >= 2 ** level_idx).astype(jnp.int32)
    return bucket

def reference(events, timestamps, norm_gain, w_in, rel_bias, out_gain, w_out):
    inputs32 = events.astype(jnp.float32)
    normed = layer_norm(inputs32, norm_gain).astype(jnp.bfloat16)
    projected = jax.nn.silu(jnp.dot(normed, w_in, preferred_element_type=jnp.float32)).astype(jnp.bfloat16)
    gate_part = projected[:, :D]
    query_part = projected[:, D:2 * D].astype(jnp.float32)
    key_part = projected[:, 2 * D:3 * D].astype(jnp.float32)
    value_part = projected[:, 3 * D:].astype(jnp.float32)
    scale_factor = 1.0 / math.sqrt(HEAD)
    positions = jnp.arange(SEQ, dtype=jnp.int32)
    pieces_out = []
    for block_idx in range(SEQ // QB):
        begin_row = block_idx * QB
        finish = begin_row + QB
        query_heads = query_part[begin_row:finish].reshape(QB, HEADS, HEAD)
        key_heads = key_part[:finish].reshape(finish, HEADS, HEAD)
        value_heads = value_part[:finish].reshape(finish, HEADS, HEAD)
        scores = jnp.einsum('qhd,khd->hqk', query_heads, key_heads) * scale_factor
        time_delta = timestamps[begin_row:finish][:, None] - timestamps[:finish][None, :]
        bias_tile = jnp.take(rel_bias, bucket_of(time_delta), axis=1)
        causal = positions[begin_row:finish][:, None] >= positions[:finish][None, :]
        weights = jnp.where(causal[None], jax.nn.silu(scores + bias_tile), 0.0).astype(jnp.bfloat16)
        attended = jnp.einsum('hqk,khd->qhd', weights.astype(jnp.float32), value_heads)
        pieces_out.append(attended.reshape(QB, D))
    attention = jnp.concatenate(pieces_out, axis=0)
    mixed_rows = (layer_norm(attention, out_gain) * gate_part.astype(jnp.float32)).astype(jnp.bfloat16)
    return (inputs32 + jnp.dot(mixed_rows, w_out, preferred_element_type=jnp.float32)).astype(jnp.bfloat16)
```

```python
import functools
import math

import jax
import jax.numpy as jnp
from jax import lax
from jax.experimental import pallas as pl
from jax.experimental.pallas import tpu as pltpu
from jax.sharding import PartitionSpec as P

HEAD = 128
NEAR = 2
LANES = 128
MESH = pl.DeviceIdType.MESH


def layer_norm(values, gain):
    center = values - jnp.mean(values, axis=-1, keepdims=True)
    variance = jnp.mean(center * center, axis=-1, keepdims=True)
    return center * lax.rsqrt(variance + 1e-05) * gain


def silu(values):
    half = 0.5 * values
    return half + half * jnp.tanh(half)


def dot(a, b):
    return jnp.dot(a, b, preferred_element_type=jnp.float32)


def kernel(
    fold, n_rows, n_cols, ev, ts_in, norm_gain_in, w_in_in, rel_bias_in, out_gain_in, w_out_in, out,
    ts, norm_gain, w_in, rel_bias, out_gain, w_out, load_sem, kv_buf, q_buf, red_buf, send_buf, q_all, q_times, acc, table, gate,
    ready, row_send, row_recv, col_send, col_recv, red_send, red_recv,
):
    axis_row, axis_cols = lax.axis_index("row"), n_cols // fold
    my_row, inner = axis_row // fold, lax.rem(axis_row, fold)
    my_col = inner * axis_cols + lax.axis_index("col")
    local, width = q_buf.shape[1:]
    heads, buckets = rel_bias.shape
    block = local * n_cols
    group = LANES // local
    tile = min(block, 512)
    near = NEAR if axis_cols % NEAR == 0 else 1
    half_scale = 0.5 / math.sqrt(HEAD)

    def in_col(r):
        return {"row": r * fold + inner}

    def in_row(c):
        return {"row": my_row * fold + c // axis_cols, "col": lax.rem(c, axis_cols)}

    barrier = pltpu.get_barrier_semaphore()

    def greet(semaphore, target):
        pl.semaphore_signal(semaphore, inc=1, device_id=target, device_id_type=MESH)

    beside = (my_row > 0) * 1 + (my_row < n_rows - 1) * 1
    part_cols = axis_cols // near
    my_part = my_col // near
    far = [
        lax.rem(inner + i, fold) * part_cols + lax.rem(my_part % part_cols + j, part_cols)
        for i in range(fold) for j in range(part_cols) if i + j > 0
    ]
    mates = [my_part * near + lax.rem(my_col % near + step, near) for step in range(1, near)]
    others = mates + [q * near + k for q in far for k in range(near)]

    @pl.when(my_row > 0)
    def _():
        greet(barrier, in_col(my_row - 1))

    @pl.when(my_row < n_rows - 1)
    def _():
        greet(barrier, in_col(my_row + 1))

    for c in others:
        greet(barrier, in_row(c))

    loads = [
        pltpu.make_async_copy(source, target, load_sem.at[i])
        for i, (source, target) in enumerate([
            (ev, q_buf.at[my_col]), (ev, kv_buf.at[my_row]), (norm_gain_in, norm_gain),
            (w_in_in, w_in), (rel_bias_in, rel_bias), (ts_in, ts),
            (out_gain_in, out_gain), (w_out_in, w_out),
        ])
    ]
    for load in loads:
        load.start()
    loads[0].wait()
    pl.semaphore_wait(barrier, beside + n_cols - 1)

    def row_copy(slot, r):
        return pltpu.make_async_remote_copy(
            src_ref=q_buf.at[my_col], dst_ref=kv_buf.at[slot], send_sem=row_send.at[r],
            recv_sem=row_recv.at[slot], device_id=in_col(r), device_id_type=MESH,
        )

    def col_copy(slot, c):
        return pltpu.make_async_remote_copy(
            src_ref=q_buf.at[my_col], dst_ref=q_buf.at[slot], send_sem=col_send.at[c],
            recv_sem=col_recv.at[slot], device_id=in_row(c), device_id_type=MESH,
        )

    def red_copy(slot, c):
        return pltpu.make_async_remote_copy(
            src_ref=send_buf.at[c], dst_ref=red_buf.at[slot], send_sem=red_send.at[c],
            recv_sem=red_recv.at[slot], device_id=in_row(c), device_id_type=MESH,
        )

    def start_row(i, carry):
        row_copy(my_row, n_rows - 1 - i).start()
        return carry

    @pl.when(my_row < n_rows - 1)
    def _():
        row_copy(my_row, my_row + 1).start()

    for c in mates + others[:len(mates) - 1:-1]:
        col_copy(my_col, c).start()

    @pl.when(my_row < n_rows - 2)
    def _():
        pl.semaphore_wait(ready, 1)

    @pl.when((my_row > 0) & (my_row < n_rows - 1))
    def _():
        greet(ready, in_col(my_row - 1))

    lax.fori_loop(0, n_rows - 2 - my_row, start_row, 0)

    for load in loads[1:]:
        load.wait()
    own = q_buf[my_col]
    lead = my_row // group * group
    for g in range(group):
        r = lead + g

        @pl.when(r > my_row)
        def _():
            kv_buf[r] = jnp.zeros_like(own)

    normed = layer_norm(own.astype(jnp.float32), norm_gain[...]).astype(jnp.bfloat16)
    gate[...] = silu(dot(normed, w_in[:, :width])).astype(jnp.bfloat16)

    lane = lax.broadcasted_iota(jnp.int32, (heads, LANES), 1)
    table[:, :buckets] = rel_bias[...]
    table[...] = 0.5 * jnp.where(lane < buckets, table[...], rel_bias[:, buckets - 1 :])
    for i in range(block // LANES):
        stamps = ts[pl.ds(my_row * (block // LANES) + i, 1), :]
        q_times[pl.ds(i * LANES, LANES), :] = jnp.broadcast_to(stamps, (LANES, LANES)).T

    def members(q):
        return mates if q is my_part else [q * near + k for k in range(near)]

    def project_queries(q):
        for c in members(q):
            col_copy(c, c).wait_recv()
        size = near * local
        rows = q_buf[pl.ds(q * near, near)].reshape(size, width).astype(jnp.float32)
        normed_q = layer_norm(rows, norm_gain[...]).astype(jnp.bfloat16)
        q_all[pl.ds(pl.multiple_of(q * size, size), size), :] = silu(
            dot(normed_q, w_in[:, width : 2 * width])
        ).astype(jnp.bfloat16)

    def each_tile(body):
        if block == tile:
            body(0)
        else:
            lax.fori_loop(0, block // tile, lambda i, carry: (body(i), carry)[1], 0)

    def chunk(c):
        return acc[pl.ds(pl.multiple_of(c * local, local), local), :]

    def send_sum(c):
        send_buf[c] = chunk(c).astype(jnp.bfloat16)
        red_copy(my_col, c).start()

    def attend(p, diagonal, tail=False):
        first = p * group
        for g in range(group):
            r = first + g
            if diagonal:

                @pl.when(r < my_row)
                def _():
                    row_copy(r, r).wait_recv()

            else:
                row_copy(r, r).wait_recv()
        rows = kv_buf[pl.ds(first, group)].reshape(LANES, width).astype(jnp.float32)
        normed_kv = layer_norm(rows, norm_gain[...]).astype(jnp.bfloat16)
        pair = silu(dot(normed_kv, w_in[:, 2 * width :])).astype(jnp.bfloat16)
        spot = lax.broadcasted_iota(jnp.int32, (1, LANES), 1)
        key_times = jnp.zeros((1, LANES), jnp.int32)
        for g in range(group):
            begin = (first + g) * block + my_col * local
            stamps = ts[pl.ds(begin // LANES, 1), :]
            shift = lax.rem(g * local - begin % LANES + LANES, LANES)
            stamps = pltpu.roll(jnp.broadcast_to(stamps, (8, LANES)), shift, 1)[:1]
            key_times = jnp.where(spot // local == g, stamps, key_times)

        def one_tile(i, size=tile):
            begin = i * size
            if not isinstance(i, int):
                begin = pl.multiple_of(begin, size)
            here = pl.ds(begin, size)
            delta = q_times[here, :] - key_times
            bucket = 32 - lax.clz(delta)
            if diagonal:
                key_pos = (first + spot // local) * block + my_col * local + spot % local
                query_pos = (
                    my_row * block + begin
                    + lax.broadcasted_iota(jnp.int32, (size, LANES), 0)
                )
                causal = query_pos >= key_pos
            for h in range(heads):
                cols = slice(h * HEAD, (h + 1) * HEAD)
                values = slice(width + h * HEAD, width + (h + 1) * HEAD)
                bias = jnp.take_along_axis(
                    jnp.broadcast_to(table[h : h + 1, :], (size, LANES)), bucket, axis=1,
                    mode="promise_in_bounds",
                )
                scores = lax.dot_general(
                    q_all[here, cols], pair[:, cols],
                    (((1,), (1,)), ((), ())), preferred_element_type=jnp.float32,
                )
                half = scores * half_scale + bias
                weights = half + half * jnp.tanh(half)
                if diagonal:
                    weights = jnp.where(causal, weights, 0.0)
                update = dot(weights.astype(jnp.bfloat16), pair[:, values])
                if diagonal:
                    acc[here, cols] = update
                else:
                    acc[here, cols] += update

        if diagonal:
            for q in [my_part] + far:
                project_queries(q)
                one_tile(q, near * local)

                @pl.when(my_row < group)
                def _():
                    for c in members(q):
                        send_sum(c)
        elif tail:
            for q in far[::-1] + [my_part]:
                one_tile(q, near * local)
                for c in members(q):
                    send_sum(c)
        else:
            each_tile(one_tile)

    last_group = my_row // group
    attend(last_group, True)

    def one_group(i, carry):
        attend(last_group - 1 - i, False)
        return carry

    lax.fori_loop(0, last_group - 1, one_group, 0)

    @pl.when(last_group > 0)
    def _():
        attend(0, False, tail=True)

    total = chunk(my_col)
    for c in others:
        red_copy(c, c).wait_recv()
        total = total + red_buf[c].astype(jnp.float32)
    mixed = layer_norm(total, out_gain[...]) * gate[...].astype(jnp.float32)
    out[...] = (
        q_buf[my_col].astype(jnp.float32) + dot(mixed.astype(jnp.bfloat16), w_out[...])
    ).astype(jnp.bfloat16)

    def end_row(i, carry):
        row_copy(my_row, n_rows - 1 - i).wait_send()
        return carry

    lax.fori_loop(0, n_rows - 1 - my_row, end_row, 0)
    for c in others:
        col_copy(my_col, c).wait_send()
        red_copy(my_col, c).wait_send()


def solution(mesh):
    fold = 2 if mesh.shape["row"] % 4 == 0 else 1
    n_rows, n_cols = mesh.shape["row"] // fold, mesh.shape["col"] * fold

    def on_device(events, timestamps, norm_gain, w_in, rel_bias, out_gain, w_out):
        local, width = events.shape
        block = local * n_cols
        heads = rel_bias.shape[0]
        vmem = pl.BlockSpec(memory_space=pltpu.VMEM)
        dma = pltpu.SemaphoreType.DMA
        return pl.pallas_call(
            functools.partial(kernel, fold, n_rows, n_cols),
            out_shape=pltpu.VMEM((local, width), jnp.bfloat16),
            in_specs=[pl.BlockSpec(memory_space=pl.ANY)] * 7,
            out_specs=vmem,
            scratch_shapes=[
                pltpu.VMEM((timestamps.shape[0] // LANES, LANES), jnp.int32),
                pltpu.VMEM((1, width), jnp.float32),
                pltpu.VMEM(w_in.shape, w_in.dtype),
                pltpu.VMEM(rel_bias.shape, rel_bias.dtype),
                pltpu.VMEM((1, width), jnp.float32),
                pltpu.VMEM(w_out.shape, w_out.dtype),
                dma((8,)),
                pltpu.VMEM((n_rows, local, width), jnp.bfloat16),
                pltpu.VMEM((n_cols, local, width), jnp.bfloat16),
                pltpu.VMEM((n_cols, local, width), jnp.bfloat16),
                pltpu.VMEM((n_cols, local, width), jnp.bfloat16),
                pltpu.VMEM((block, width), jnp.bfloat16),
                pltpu.VMEM((block, LANES), jnp.int32),
                pltpu.VMEM((block, width), jnp.float32),
                pltpu.VMEM((heads, LANES), jnp.float32),
                pltpu.VMEM((local, width), jnp.bfloat16),
                pltpu.SemaphoreType.REGULAR,
                dma((n_rows,)), dma((n_rows,)),
                dma((n_cols,)), dma((n_cols,)),
                dma((n_cols,)), dma((n_cols,)),
            ],
            compiler_params=pltpu.CompilerParams(collective_id=0, has_side_effects=True),
        )(
            events,
            timestamps.reshape(-1, LANES),
            norm_gain.reshape(1, -1),
            w_in,
            rel_bias,
            out_gain.reshape(1, -1),
            w_out,
        )

    return jax.shard_map(
        on_device,
        mesh=mesh,
        in_specs=(P(("row", "col"), None), P(), P(), P(), P(), P(), P()),
        out_specs=P(("row", "col"), None),
        check_vma=False,
    )
```

```python
import functools
import math

import jax
import jax.numpy as jnp
from jax import lax
from jax.experimental import pallas as pl
from jax.experimental.pallas import tpu as pltpu
from jax.sharding import PartitionSpec as P

HEAD = 128
CORES = 2
LANES = 128
MESH = pl.DeviceIdType.MESH


def layer_norm(values, gain):
    center = values - jnp.mean(values, axis=-1, keepdims=True)
    variance = jnp.mean(center * center, axis=-1, keepdims=True)
    return center * lax.rsqrt(variance + 1e-05) * gain


def silu(values):
    half = 0.5 * values
    return half + half * jnp.tanh(half)


def dot(a, b):
    return jnp.dot(a, b, preferred_element_type=jnp.float32)


def kernel(
    fold, n_rows, n_cols, ev, ts_in, norm_gain_in, w_in_in, rel_bias_in, out_gain_in, w_out_in, out,
    raw, ts, norm_gain, w_in, rel_bias, out_gain, w_out, load_sem,
    plane_buf, query_buf, red_buf, send_buf, pair_buf, q_times, total, table, gate, ready,
    plane_send, plane_recv, hand_send, hand_recv, query_send, query_recv, red_send, red_recv,
):
    axis_row, axis_col = lax.axis_index("row"), lax.axis_index("col")
    n_chips = n_cols // CORES
    side = n_chips // fold
    plane, inner = axis_row // fold, lax.rem(axis_row, fold)
    core, place = lax.rem(axis_col, CORES), axis_col // CORES
    other = 1 - core
    chip = inner * side + place
    local, width = raw.shape
    heads, buckets = rel_bias.shape
    later_planes, later_chips = n_rows - 1 - plane, n_chips - 1 - chip
    group = min(n_chips, 4)
    half_scale = 0.5 / math.sqrt(HEAD)

    peers = [
        lax.rem(inner + i, fold) * side + lax.rem(place + j, side)
        for i in range(fold) for j in range(side) if i + j > 0
    ]

    def in_plane(i):
        return {"row": plane * fold + i // side, "col": lax.rem(i, side) * CORES + other}

    def in_column(r):
        return {"row": r * fold + inner, "col": place * CORES + other}

    partner = {"row": axis_row, "col": place * CORES + other}

    def each(count, body):
        lax.fori_loop(0, count, lambda i, carry: (body(i), carry)[1], 0)

    barrier = pltpu.get_barrier_semaphore()

    def greet(semaphore, target):
        pl.semaphore_signal(semaphore, inc=1, device_id=target, device_id_type=MESH)

    each(later_planes, lambda i: greet(barrier, in_column(n_rows - 1 - i)))
    each(later_chips, lambda i: greet(barrier, in_plane(n_chips - 1 - i)))
    greet(barrier, partner)

    loads = [
        pltpu.make_async_copy(source, target, load_sem.at[i])
        for i, (source, target) in enumerate([
            (ev, raw), (norm_gain_in, norm_gain), (ts_in, ts), (rel_bias_in, rel_bias), (w_in_in, w_in),
            (out_gain_in, out_gain), (w_out_in, w_out),
        ])
    ]
    for load in loads:
        load.start()

    def remote(source, target, send_sem, recv_sem, device):
        return pltpu.make_async_remote_copy(
            src_ref=source, dst_ref=target, send_sem=send_sem, recv_sem=recv_sem,
            device_id=device, device_id_type=MESH,
        )

    mine = plane_buf.at[chip, core]

    def plane_copy(slot, i):
        return remote(mine, plane_buf.at[slot, core], plane_send.at[i], plane_recv.at[slot], in_plane(i))

    def query_copy(slot, r):
        return remote(mine, query_buf.at[slot], query_send.at[r], query_recv.at[slot], in_column(r))

    own_hand = remote(mine, mine, hand_send.at[chip], hand_recv.at[chip], partner)

    def hand(i):
        return remote(plane_buf.at[i, other], plane_buf.at[i, other], hand_send.at[i], hand_recv.at[i], partner)

    def red_copy(slot, r):
        return remote(send_buf.at[r], red_buf.at[slot], red_send.at[r], red_recv.at[slot], in_column(r))

    pl.semaphore_wait(barrier, plane + chip + 1)
    each(chip, lambda i: greet(ready, in_plane(i)))

    loads[0].wait()
    loads[1].wait()
    own = layer_norm(raw[...].astype(jnp.float32), norm_gain[...]).astype(jnp.bfloat16)
    plane_buf[chip, core] = own

    each(plane, lambda r: query_copy(plane, r).start())
    each(chip, lambda i: plane_copy(chip, i).start())
    own_hand.start()

    for load in loads[2:4]:
        load.wait()

    lane = lax.broadcasted_iota(jnp.int32, (heads, LANES), 1)
    table[:, :buckets] = rel_bias[...]
    table[...] = 0.5 * jnp.where(lane < buckets, table[...], rel_bias[:, buckets - 1 :])

    def stamps_of(r, i):
        return ts[pl.ds(r * n_chips + i, 1), :]

    def fill_times(r, part):
        stamps = jnp.broadcast_to(stamps_of(r, chip), (LANES, LANES)).T
        q_times[r] = jnp.where(part > 0, stamps[local:], stamps[:local])

    fill_times(plane, core)
    each(later_planes, lambda i: fill_times(plane + 1 + i, other))

    @pl.when(later_chips > 0)
    def _():
        pl.semaphore_wait(ready, later_chips)

    each(later_chips, lambda i: plane_copy(chip, n_chips - 1 - i).start())

    for load in loads[4:]:
        load.wait()

    def project_query(rows):
        return silu(dot(rows, w_in[:, width : 2 * width])).astype(jnp.bfloat16)

    def project_pair(i):
        rows = pl.ds(pl.multiple_of(i * LANES, LANES), LANES)
        block = plane_buf[i].reshape(LANES, width)
        pair_buf[rows, :] = silu(dot(block, w_in[:, 2 * width :])).astype(jnp.bfloat16)

    def attend(query, times, causal):
        def keys(first):
            rows = pl.ds(pl.multiple_of(first * LANES, LANES), group * LANES)
            buckets_of = [32 - lax.clz(times - stamps_of(plane, first + i)) for i in range(group)]
            if causal:
                query_pos = chip * LANES + core * local + lax.broadcasted_iota(jnp.int32, (local, group * LANES), 0)
                key_pos = first * LANES + lax.broadcasted_iota(jnp.int32, (local, group * LANES), 1)
            parts = []
            for h in range(heads):
                cols = slice(h * HEAD, (h + 1) * HEAD)
                values = slice(width + h * HEAD, width + (h + 1) * HEAD)
                row = jnp.broadcast_to(table[h : h + 1, :], (local, LANES))
                bias = jnp.concatenate([
                    jnp.take_along_axis(row, bucket, axis=1, mode="promise_in_bounds")
                    for bucket in buckets_of
                ], axis=1)
                scores = lax.dot_general(
                    query[:, cols], pair_buf[rows, cols],
                    (((1,), (1,)), ((), ())), preferred_element_type=jnp.float32,
                )
                half = scores * half_scale + bias
                weights = half + half * jnp.tanh(half)
                if causal:
                    weights = jnp.where(query_pos >= key_pos, weights, 0.0)
                parts.append(dot(weights.astype(jnp.bfloat16), pair_buf[rows, values]))
            return jnp.concatenate(parts, axis=1)

        if group == n_chips:
            return keys(0)
        return lax.fori_loop(
            0, n_chips // group, lambda g, sums: sums + keys(g * group),
            jnp.zeros((local, width), jnp.float32),
        )

    own_query = project_query(own)
    gate[...] = silu(dot(own, w_in[:, :width])).astype(jnp.bfloat16)

    own_hand.wait_recv()
    project_pair(chip)
    for i in peers:
        plane_copy(i, i).wait_recv()
        hand(i).start()
    for i in peers:
        hand(i).wait_recv()
        project_pair(i)

    def serve(i):
        r = plane + 1 + i
        query_copy(r, r).wait_recv()
        query = project_query(query_buf[r])
        send_buf[r] = attend(query, q_times[r], False).astype(jnp.bfloat16)
        red_copy(plane, r).start()

    each(later_planes, serve)
    total[...] = attend(own_query, q_times[plane], True)

    def gather(r):
        red_copy(r, r).wait_recv()
        total[...] += red_buf[r].astype(jnp.float32)

    each(plane, gather)

    mixed = layer_norm(total[...], out_gain[...]) * gate[...].astype(jnp.float32)
    out[...] = (
        raw[...].astype(jnp.float32) + dot(mixed.astype(jnp.bfloat16), w_out[...])
    ).astype(jnp.bfloat16)

    own_hand.wait_send()
    for i in peers:
        plane_copy(chip, i).wait_send()
        hand(i).wait_send()
    each(plane, lambda r: query_copy(plane, r).wait_send())
    each(later_planes, lambda i: red_copy(plane, plane + 1 + i).wait_send())


def solution(mesh):
    fold = 2 if mesh.shape["row"] % 4 == 0 else 1
    n_rows, n_cols = mesh.shape["row"] // fold, mesh.shape["col"] * fold
    n_chips = n_cols // CORES

    def on_device(events, timestamps, norm_gain, w_in, rel_bias, out_gain, w_out):
        local, width = events.shape
        if local * CORES != LANES or mesh.shape["col"] % CORES:
            raise ValueError("unsupported sizes")
        heads = rel_bias.shape[0]
        vmem = pl.BlockSpec(memory_space=pltpu.VMEM)
        dma = pltpu.SemaphoreType.DMA
        return pl.pallas_call(
            functools.partial(kernel, fold, n_rows, n_cols),
            out_shape=pltpu.VMEM((local, width), jnp.bfloat16),
            in_specs=[pl.BlockSpec(memory_space=pl.ANY)] * 7,
            out_specs=vmem,
            scratch_shapes=[
                pltpu.VMEM((local, width), jnp.bfloat16),
                pltpu.VMEM((timestamps.shape[0] // LANES, LANES), jnp.int32),
                pltpu.VMEM((1, width), jnp.float32),
                pltpu.VMEM(w_in.shape, w_in.dtype),
                pltpu.VMEM(rel_bias.shape, rel_bias.dtype),
                pltpu.VMEM((1, width), jnp.float32),
                pltpu.VMEM(w_out.shape, w_out.dtype),
                dma((7,)),
                pltpu.VMEM((n_chips, CORES, local, width), jnp.bfloat16),
                pltpu.VMEM((n_rows, local, width), jnp.bfloat16),
                pltpu.VMEM((n_rows, local, width), jnp.bfloat16),
                pltpu.VMEM((n_rows, local, width), jnp.bfloat16),
                pltpu.VMEM((n_chips * LANES, 2 * width), jnp.bfloat16),
                pltpu.VMEM((n_rows, local, LANES), jnp.int32),
                pltpu.VMEM((local, width), jnp.float32),
                pltpu.VMEM((heads, LANES), jnp.float32),
                pltpu.VMEM((local, width), jnp.bfloat16),
                pltpu.SemaphoreType.REGULAR,
                dma((n_chips,)), dma((n_chips,)), dma((n_chips,)), dma((n_chips,)),
                dma((n_rows,)), dma((n_rows,)), dma((n_rows,)), dma((n_rows,)),
            ],
            compiler_params=pltpu.CompilerParams(collective_id=0, has_side_effects=True),
        )(
            events,
            timestamps.reshape(-1, LANES),
            norm_gain.reshape(1, -1),
            w_in,
            rel_bias,
            out_gain.reshape(1, -1),
            w_out,
        )

    return jax.shard_map(
        on_device,
        mesh=mesh,
        in_specs=(P(("row", "col"), None), P(), P(), P(), P(), P(), P()),
        out_specs=P(("row", "col"), None),
        check_vma=False,
    )
```

```python
import functools
import math

import jax
import jax.numpy as jnp
from jax import lax
from jax.experimental import pallas as pl
from jax.experimental.pallas import tpu as pltpu
from jax.sharding import PartitionSpec as P

HEAD = 128
CORES = 2
LANES = 128
MESH = pl.DeviceIdType.MESH


def layer_norm(values, gain):
    center = values - jnp.mean(values, axis=-1, keepdims=True)
    variance = jnp.mean(center * center, axis=-1, keepdims=True)
    return center * lax.rsqrt(variance + 1e-05) * gain


def silu(values):
    half = 0.5 * values
    return half + half * jnp.tanh(half)


def dot(a, b):
    return jnp.dot(a, b, preferred_element_type=jnp.float32)


def kernel(
    fold, n_rows, n_cols, ev, ts_in, norm_gain_in, w_in_in, rel_bias_in, out_gain_in, w_out_in, out,
    raw, ts, norm_gain, w_in, rel_bias, out_gain, w_out, load_sem,
    plane_buf, query_buf, red_buf, send_buf, pair_buf, q_times, total, table, gate, ready,
    plane_send, plane_recv, hand_send, hand_recv, query_send, query_recv, red_send, red_recv,
):
    axis_row, axis_col = lax.axis_index("row"), lax.axis_index("col")
    n_chips = n_cols // CORES
    side = n_chips // fold
    plane, inner = axis_row // fold, lax.rem(axis_row, fold)
    core, place = lax.rem(axis_col, CORES), axis_col // CORES
    other = 1 - core
    chip = inner * side + place
    local, width = raw.shape
    heads, buckets = rel_bias.shape
    later_planes = n_rows - 1 - plane
    group = min(n_chips, 4)
    half_scale = 0.5 / math.sqrt(HEAD)

    peers = [
        lax.rem(inner + i, fold) * side + lax.rem(place + j, side)
        for i in range(fold) for j in range(side) if i + j > 0
    ]

    def in_plane(i, member=other):
        return {"row": plane * fold + i // side, "col": lax.rem(i, side) * CORES + member}

    def in_column(r, member=other):
        return {"row": r * fold + inner, "col": place * CORES + member}

    partner = {"row": axis_row, "col": place * CORES + other}

    def each(count, body):
        lax.fori_loop(0, count, lambda i, carry: (body(i), carry)[1], 0)

    barrier = pltpu.get_barrier_semaphore()

    def greet(semaphore, target):
        pl.semaphore_signal(semaphore, inc=1, device_id=target, device_id_type=MESH)

    for i in peers[::-1]:
        greet(barrier, in_plane(i, 1))
    each(later_planes, lambda i: greet(barrier, in_column(n_rows - 1 - i, 0)))

    @pl.when(core == 1)
    def _():
        greet(barrier, partner)

    loads = [
        pltpu.make_async_copy(source, target, load_sem.at[i])
        for i, (source, target) in enumerate([
            (ev, raw), (norm_gain_in, norm_gain), (ts_in, ts), (rel_bias_in, rel_bias), (w_in_in, w_in),
            (out_gain_in, out_gain), (w_out_in, w_out),
        ])
    ]
    for load in loads:
        load.start()

    def remote(source, target, send_sem, recv_sem, device):
        return pltpu.make_async_remote_copy(
            src_ref=source, dst_ref=target, send_sem=send_sem, recv_sem=recv_sem,
            device_id=device, device_id_type=MESH,
        )

    mine = plane_buf.at[chip, core]

    def plane_copy(slot, i):
        return remote(mine, plane_buf.at[slot, core], plane_send.at[i], plane_recv.at[slot], in_plane(i))

    def query_copy(slot, r):
        return remote(mine, query_buf.at[slot], query_send.at[r], query_recv.at[slot], in_column(r))

    own_hand = remote(mine, mine, hand_send.at[chip], hand_recv.at[chip], partner)

    def hand(i):
        return remote(plane_buf.at[i, other], plane_buf.at[i, other], hand_send.at[i], hand_recv.at[i], partner)

    def red_copy(slot, r):
        return remote(send_buf.at[r], red_buf.at[slot], red_send.at[r], red_recv.at[slot], in_column(r))

    @pl.when(core == 0)
    def _():
        pl.semaphore_wait(barrier, CORES * plane + 1)
        greet(ready, partner)

    loads[0].wait()
    loads[1].wait()
    own = layer_norm(raw[...].astype(jnp.float32), norm_gain[...]).astype(jnp.bfloat16)
    plane_buf[chip, core] = own

    @pl.when(core == 1)
    def _():
        pl.semaphore_wait(ready, 1)

    each(plane, lambda r: query_copy(plane, r).start())
    own_hand.start()

    @pl.when(core == 1)
    def _():
        pl.semaphore_wait(barrier, CORES * (n_chips - 1))
        greet(ready, partner)

    @pl.when(core == 0)
    def _():
        pl.semaphore_wait(ready, 1)

    for i in peers[::-1]:
        plane_copy(chip, i).start()

    for load in loads[2:4]:
        load.wait()

    lane = lax.broadcasted_iota(jnp.int32, (heads, LANES), 1)
    table[:, :buckets] = rel_bias[...]
    table[...] = 0.5 * jnp.where(lane < buckets, table[...], rel_bias[:, buckets - 1 :])

    def stamps_of(r, i):
        return ts[pl.ds(r * n_chips + i, 1), :]

    def fill_times(r, part):
        stamps = jnp.broadcast_to(stamps_of(r, chip), (LANES, LANES)).T
        q_times[r] = jnp.where(part > 0, stamps[local:], stamps[:local])

    fill_times(plane, core)
    each(later_planes, lambda i: fill_times(plane + 1 + i, other))

    for load in loads[4:]:
        load.wait()

    def project_query(rows):
        return silu(dot(rows, w_in[:, width : 2 * width])).astype(jnp.bfloat16)

    def project_pair(i):
        rows = pl.ds(pl.multiple_of(i * LANES, LANES), LANES)
        block = plane_buf[i].reshape(LANES, width)
        pair_buf[rows, :] = silu(dot(block, w_in[:, 2 * width :])).astype(jnp.bfloat16)

    def attend(query, times, causal):
        def keys(first):
            rows = pl.ds(pl.multiple_of(first * LANES, LANES), group * LANES)
            buckets_of = [32 - lax.clz(times - stamps_of(plane, first + i)) for i in range(group)]
            if causal:
                query_pos = chip * LANES + core * local + lax.broadcasted_iota(jnp.int32, (local, group * LANES), 0)
                key_pos = first * LANES + lax.broadcasted_iota(jnp.int32, (local, group * LANES), 1)
            parts = []
            for h in range(heads):
                cols = slice(h * HEAD, (h + 1) * HEAD)
                values = slice(width + h * HEAD, width + (h + 1) * HEAD)
                row = jnp.broadcast_to(table[h : h + 1, :], (local, LANES))
                bias = jnp.concatenate([
                    jnp.take_along_axis(row, bucket, axis=1, mode="promise_in_bounds")
                    for bucket in buckets_of
                ], axis=1)
                scores = lax.dot_general(
                    query[:, cols], pair_buf[rows, cols],
                    (((1,), (1,)), ((), ())), preferred_element_type=jnp.float32,
                )
                half = scores * half_scale + bias
                weights = half + half * jnp.tanh(half)
                if causal:
                    weights = jnp.where(query_pos >= key_pos, weights, 0.0)
                parts.append(dot(weights.astype(jnp.bfloat16), pair_buf[rows, values]))
            return jnp.concatenate(parts, axis=1)

        if group == n_chips:
            return keys(0)
        return lax.fori_loop(
            0, n_chips // group, lambda g, sums: sums + keys(g * group),
            jnp.zeros((local, width), jnp.float32),
        )

    own_query = project_query(own)
    gate[...] = silu(dot(own, w_in[:, :width])).astype(jnp.bfloat16)

    own_hand.wait_recv()
    project_pair(chip)
    for i in peers:
        plane_copy(i, i).wait_recv()
        hand(i).start()
    for i in peers:
        hand(i).wait_recv()
        project_pair(i)

    def serve(i):
        r = plane + 1 + i
        query_copy(r, r).wait_recv()
        query = project_query(query_buf[r])
        send_buf[r] = attend(query, q_times[r], False).astype(jnp.bfloat16)
        red_copy(plane, r).start()

    @pl.when(later_planes > 0)
    def _():
        serve(later_planes - 1)

    each(later_planes - 1, serve)
    total[...] = attend(own_query, q_times[plane], True)

    def gather(r):
        red_copy(r, r).wait_recv()
        total[...] += red_buf[r].astype(jnp.float32)

    each(plane, gather)

    mixed = layer_norm(total[...], out_gain[...]) * gate[...].astype(jnp.float32)
    out[...] = (
        raw[...].astype(jnp.float32) + dot(mixed.astype(jnp.bfloat16), w_out[...])
    ).astype(jnp.bfloat16)

    own_hand.wait_send()
    for i in peers:
        plane_copy(chip, i).wait_send()
        hand(i).wait_send()
    each(plane, lambda r: query_copy(plane, r).wait_send())
    each(later_planes, lambda i: red_copy(plane, plane + 1 + i).wait_send())


def solution(mesh):
    fold = 2 if mesh.shape["row"] % 4 == 0 else 1
    n_rows, n_cols = mesh.shape["row"] // fold, mesh.shape["col"] * fold
    n_chips = n_cols // CORES

    def on_device(events, timestamps, norm_gain, w_in, rel_bias, out_gain, w_out):
        local, width = events.shape
        if local * CORES != LANES or mesh.shape["col"] % CORES:
            raise ValueError("unsupported sizes")
        heads = rel_bias.shape[0]
        vmem = pl.BlockSpec(memory_space=pltpu.VMEM)
        dma = pltpu.SemaphoreType.DMA
        return pl.pallas_call(
            functools.partial(kernel, fold, n_rows, n_cols),
            out_shape=pltpu.VMEM((local, width), jnp.bfloat16),
            in_specs=[pl.BlockSpec(memory_space=pl.ANY)] * 7,
            out_specs=vmem,
            scratch_shapes=[
                pltpu.VMEM((local, width), jnp.bfloat16),
                pltpu.VMEM((timestamps.shape[0] // LANES, LANES), jnp.int32),
                pltpu.VMEM((1, width), jnp.float32),
                pltpu.VMEM(w_in.shape, w_in.dtype),
                pltpu.VMEM(rel_bias.shape, rel_bias.dtype),
                pltpu.VMEM((1, width), jnp.float32),
                pltpu.VMEM(w_out.shape, w_out.dtype),
                dma((7,)),
                pltpu.VMEM((n_chips, CORES, local, width), jnp.bfloat16),
                pltpu.VMEM((n_rows, local, width), jnp.bfloat16),
                pltpu.VMEM((n_rows, local, width), jnp.bfloat16),
                pltpu.VMEM((n_rows, local, width), jnp.bfloat16),
                pltpu.VMEM((n_chips * LANES, 2 * width), jnp.bfloat16),
                pltpu.VMEM((n_rows, local, LANES), jnp.int32),
                pltpu.VMEM((local, width), jnp.float32),
                pltpu.VMEM((heads, LANES), jnp.float32),
                pltpu.VMEM((local, width), jnp.bfloat16),
                pltpu.SemaphoreType.REGULAR,
                dma((n_chips,)), dma((n_chips,)), dma((n_chips,)), dma((n_chips,)),
                dma((n_rows,)), dma((n_rows,)), dma((n_rows,)), dma((n_rows,)),
            ],
            compiler_params=pltpu.CompilerParams(collective_id=0, has_side_effects=True),
        )(
            events,
            timestamps.reshape(-1, LANES),
            norm_gain.reshape(1, -1),
            w_in,
            rel_bias,
            out_gain.reshape(1, -1),
            w_out,
        )

    return jax.shard_map(
        on_device,
        mesh=mesh,
        in_specs=(P(("row", "col"), None), P(), P(), P(), P(), P(), P()),
        out_specs=P(("row", "col"), None),
        check_vma=False,
    )
```

```python
import functools
import math

import jax
import jax.numpy as jnp
from jax import lax
from jax.experimental import pallas as pl
from jax.experimental.pallas import tpu as pltpu
from jax.sharding import PartitionSpec as P

HEAD = 128
CORES = 2
LANES = 128
MESH = pl.DeviceIdType.MESH


def layer_norm(values, gain):
    center = values - jnp.mean(values, axis=-1, keepdims=True)
    variance = jnp.mean(center * center, axis=-1, keepdims=True)
    return center * lax.rsqrt(variance + 1e-05) * gain


def silu(values):
    half = 0.5 * values
    return half + half * jnp.tanh(half)


def dot(a, b):
    return jnp.dot(a, b, preferred_element_type=jnp.float32)


def kernel(
    fold, n_rows, n_cols, ev, ts_in, norm_gain_in, w_in_in, rel_bias_in, out_gain_in, w_out_in, out,
    raw, ts, norm_gain, w_in, rel_bias, out_gain, w_out, load_sem,
    plane_buf, query_buf, red_buf, send_buf, pair_buf, q_times, total, table, gate, ready,
    plane_send, plane_recv, hand_send, hand_recv, query_send, query_recv, red_send, red_recv,
):
    axis_row, axis_col = lax.axis_index("row"), lax.axis_index("col")
    n_chips = n_cols // CORES
    side = n_chips // fold
    plane, inner = axis_row // fold, lax.rem(axis_row, fold)
    core, place = lax.rem(axis_col, CORES), axis_col // CORES
    other = 1 - core
    chip = inner * side + place
    local, width = raw.shape
    heads, buckets = rel_bias.shape
    later_planes = n_rows - 1 - plane
    group = min(n_chips, 4)
    half_scale = 0.5 / math.sqrt(HEAD)

    peers = [
        lax.rem(inner + i, fold) * side + lax.rem(place + j, side)
        for i in range(fold) for j in range(side) if i + j > 0
    ]

    def in_plane(i, member=other):
        return {"row": plane * fold + i // side, "col": lax.rem(i, side) * CORES + member}

    def in_column(r, member=other):
        return {"row": r * fold + inner, "col": place * CORES + member}

    partner = {"row": axis_row, "col": place * CORES + other}

    def each(count, body):
        lax.fori_loop(0, count, lambda i, carry: (body(i), carry)[1], 0)

    barrier = pltpu.get_barrier_semaphore()

    def greet(semaphore, target):
        pl.semaphore_signal(semaphore, inc=1, device_id=target, device_id_type=MESH)

    for i in peers[::-1]:
        greet(barrier, in_plane(i, 1))
    each(later_planes, lambda i: greet(barrier, in_column(n_rows - 1 - i, 0)))

    @pl.when(core == 1)
    def _():
        greet(barrier, partner)

    loads = [
        pltpu.make_async_copy(source, target, load_sem.at[i])
        for i, (source, target) in enumerate([
            (ev, raw), (norm_gain_in, norm_gain), (w_in_in, w_in), (ts_in, ts), (rel_bias_in, rel_bias),
            (out_gain_in, out_gain), (w_out_in, w_out),
        ])
    ]
    for load in loads:
        load.start()

    def remote(source, target, send_sem, recv_sem, device):
        return pltpu.make_async_remote_copy(
            src_ref=source, dst_ref=target, send_sem=send_sem, recv_sem=recv_sem,
            device_id=device, device_id_type=MESH,
        )

    mine = plane_buf.at[chip, core]

    def plane_copy(slot, i):
        return remote(mine, plane_buf.at[slot, core], plane_send.at[i], plane_recv.at[slot], in_plane(i))

    def query_copy(slot, r):
        return remote(query_buf.at[plane], query_buf.at[slot], query_send.at[r], query_recv.at[slot], in_column(r))

    own_hand = remote(mine, mine, hand_send.at[chip], hand_recv.at[chip], partner)

    def hand(i):
        return remote(plane_buf.at[i, other], plane_buf.at[i, other], hand_send.at[i], hand_recv.at[i], partner)

    def red_copy(slot, r):
        return remote(send_buf.at[r], red_buf.at[slot], red_send.at[r], red_recv.at[slot], in_column(r))

    @pl.when(core == 0)
    def _():
        pl.semaphore_wait(barrier, CORES * plane + 1)
        greet(ready, partner)

    loads[0].wait()
    loads[1].wait()
    own = layer_norm(raw[...].astype(jnp.float32), norm_gain[...]).astype(jnp.bfloat16)
    plane_buf[chip, core] = own

    @pl.when(core == 1)
    def _():
        pl.semaphore_wait(ready, 1)

    def project_query(rows):
        return silu(dot(rows, w_in[:, width : 2 * width])).astype(jnp.bfloat16)

    own_hand.start()
    loads[2].wait()
    query_buf[plane] = project_query(own)
    each(plane, lambda r: query_copy(plane, r).start())
    @pl.when(core == 1)
    def _():
        pl.semaphore_wait(barrier, CORES * (n_chips - 1))
        greet(ready, partner)

    @pl.when(core == 0)
    def _():
        pl.semaphore_wait(ready, 1)

    for i in peers[::-1]:
        plane_copy(chip, i).start()

    for load in loads[3:5]:
        load.wait()

    lane = lax.broadcasted_iota(jnp.int32, (heads, LANES), 1)
    table[:, :buckets] = rel_bias[...]
    table[...] = 0.5 * jnp.where(lane < buckets, table[...], rel_bias[:, buckets - 1 :])

    def stamps_of(r, i):
        return ts[pl.ds(r * n_chips + i, 1), :]

    def fill_times(r, part):
        stamps = jnp.broadcast_to(stamps_of(r, chip), (LANES, LANES)).T
        q_times[r] = jnp.where(part > 0, stamps[local:], stamps[:local])

    fill_times(plane, core)
    each(later_planes, lambda i: fill_times(plane + 1 + i, other))

    for load in loads[5:]:
        load.wait()

    def project_pair(i):
        rows = pl.ds(pl.multiple_of(i * LANES, LANES), LANES)
        block = plane_buf[i].reshape(LANES, width)
        pair_buf[rows, :] = silu(dot(block, w_in[:, 2 * width :])).astype(jnp.bfloat16)

    def attend(query, times, causal):
        def keys(first):
            rows = pl.ds(pl.multiple_of(first * LANES, LANES), group * LANES)
            buckets_of = [32 - lax.clz(times - stamps_of(plane, first + i)) for i in range(group)]
            if causal:
                query_pos = chip * LANES + core * local + lax.broadcasted_iota(jnp.int32, (local, group * LANES), 0)
                key_pos = first * LANES + lax.broadcasted_iota(jnp.int32, (local, group * LANES), 1)
            parts = []
            for h in range(heads):
                cols = slice(h * HEAD, (h + 1) * HEAD)
                values = slice(width + h * HEAD, width + (h + 1) * HEAD)
                row = jnp.broadcast_to(table[h : h + 1, :], (local, LANES))
                bias = jnp.concatenate([
                    jnp.take_along_axis(row, bucket, axis=1, mode="promise_in_bounds")
                    for bucket in buckets_of
                ], axis=1)
                scores = lax.dot_general(
                    query[:, cols], pair_buf[rows, cols],
                    (((1,), (1,)), ((), ())), preferred_element_type=jnp.float32,
                )
                half = scores * half_scale + bias
                weights = half + half * jnp.tanh(half)
                if causal:
                    weights = jnp.where(query_pos >= key_pos, weights, 0.0)
                parts.append(dot(weights.astype(jnp.bfloat16), pair_buf[rows, values]))
            return jnp.concatenate(parts, axis=1)

        if group == n_chips:
            return keys(0)
        return lax.fori_loop(
            0, n_chips // group, lambda g, sums: sums + keys(g * group),
            jnp.zeros((local, width), jnp.float32),
        )

    gate[...] = silu(dot(own, w_in[:, :width])).astype(jnp.bfloat16)

    own_hand.wait_recv()
    project_pair(chip)
    for i in peers:
        plane_copy(i, i).wait_recv()
        hand(i).start()
    for i in peers:
        hand(i).wait_recv()
        project_pair(i)

    def serve(i):
        r = plane + 1 + i
        query_copy(r, r).wait_recv()
        send_buf[r] = attend(query_buf[r], q_times[r], False).astype(jnp.bfloat16)
        red_copy(plane, r).start()

    @pl.when(later_planes > 0)
    def _():
        serve(later_planes - 1)

    each(later_planes - 1, serve)
    total[...] = attend(query_buf[plane], q_times[plane], True)

    def gather(r):
        red_copy(r, r).wait_recv()
        total[...] += red_buf[r].astype(jnp.float32)

    each(plane, gather)

    mixed = layer_norm(total[...], out_gain[...]) * gate[...].astype(jnp.float32)
    out[...] = (
        raw[...].astype(jnp.float32) + dot(mixed.astype(jnp.bfloat16), w_out[...])
    ).astype(jnp.bfloat16)

    own_hand.wait_send()
    for i in peers:
        plane_copy(chip, i).wait_send()
        hand(i).wait_send()
    each(plane, lambda r: query_copy(plane, r).wait_send())
    each(later_planes, lambda i: red_copy(plane, plane + 1 + i).wait_send())


def solution(mesh):
    fold = 2 if mesh.shape["row"] % 4 == 0 else 1
    n_rows, n_cols = mesh.shape["row"] // fold, mesh.shape["col"] * fold
    n_chips = n_cols // CORES

    def on_device(events, timestamps, norm_gain, w_in, rel_bias, out_gain, w_out):
        local, width = events.shape
        if local * CORES != LANES or mesh.shape["col"] % CORES:
            raise ValueError("unsupported sizes")
        heads = rel_bias.shape[0]
        vmem = pl.BlockSpec(memory_space=pltpu.VMEM)
        dma = pltpu.SemaphoreType.DMA
        return pl.pallas_call(
            functools.partial(kernel, fold, n_rows, n_cols),
            out_shape=pltpu.VMEM((local, width), jnp.bfloat16),
            in_specs=[pl.BlockSpec(memory_space=pl.ANY)] * 7,
            out_specs=vmem,
            scratch_shapes=[
                pltpu.VMEM((local, width), jnp.bfloat16),
                pltpu.VMEM((timestamps.shape[0] // LANES, LANES), jnp.int32),
                pltpu.VMEM((1, width), jnp.float32),
                pltpu.VMEM(w_in.shape, w_in.dtype),
                pltpu.VMEM(rel_bias.shape, rel_bias.dtype),
                pltpu.VMEM((1, width), jnp.float32),
                pltpu.VMEM(w_out.shape, w_out.dtype),
                dma((7,)),
                pltpu.VMEM((n_chips, CORES, local, width), jnp.bfloat16),
                pltpu.VMEM((n_rows, local, width), jnp.bfloat16),
                pltpu.VMEM((n_rows, local, width), jnp.bfloat16),
                pltpu.VMEM((n_rows, local, width), jnp.bfloat16),
                pltpu.VMEM((n_chips * LANES, 2 * width), jnp.bfloat16),
                pltpu.VMEM((n_rows, local, LANES), jnp.int32),
                pltpu.VMEM((local, width), jnp.float32),
                pltpu.VMEM((heads, LANES), jnp.float32),
                pltpu.VMEM((local, width), jnp.bfloat16),
                pltpu.SemaphoreType.REGULAR,
                dma((n_chips,)), dma((n_chips,)), dma((n_chips,)), dma((n_chips,)),
                dma((n_rows,)), dma((n_rows,)), dma((n_rows,)), dma((n_rows,)),
            ],
            compiler_params=pltpu.CompilerParams(collective_id=0, has_side_effects=True),
        )(
            events,
            timestamps.reshape(-1, LANES),
            norm_gain.reshape(1, -1),
            w_in,
            rel_bias,
            out_gain.reshape(1, -1),
            w_out,
        )

    return jax.shard_map(
        on_device,
        mesh=mesh,
        in_specs=(P(("row", "col"), None), P(), P(), P(), P(), P(), P()),
        out_specs=P(("row", "col"), None),
        check_vma=False,
    )
```
